32 devices in a mesh: seq: 8 (over y, x, core), fsdp: 4 (over z).
Axes of the slice: x: 2, y: 2, z: 4, core: 2. Of those that a mesh axis runs over, the one named last changes fastest.
Arguments:
- block_input: bfloat16 [4, 1024, 1024], P('fsdp', 'seq'), may hold values from -6 to 6
- doc_ids: int32 [4, 1024], replicated, may hold values from 0 to 3, never falling along the last dimension, each value on 1 to 512 neighbouring positions
- gain_attn: bfloat16 [1024], replicated, may hold values from 0.5 to 1.5
- gain_mlp: bfloat16 [1024], replicated, may hold values from 0.5 to 1.5
- w_qkv: bfloat16 [1024, 3, 1024], P(None, None, 'fsdp'), may hold values from -8 to 8
- w_out: bfloat16 [1024, 1024], P('fsdp'), may hold values from -1.5 to 1.5
- w_in: bfloat16 [1024, 2, 2624], P(None, None, 'fsdp'), may hold values from -0.1875 to 0.1875
- w_down: bfloat16 [2624, 1024], P('fsdp'), may hold values from -0.125 to 0.125
- out_grad: bfloat16 [4, 1024, 1024], P('fsdp', 'seq'), may hold values from -6 to 6
Outputs:
- output: bfloat16 [4, 1024, 1024], P('fsdp', 'seq')
- grad_input: float32 [4, 1024, 1024], P('fsdp', 'seq')
- grad_qkv: float32 [1024, 3, 1024], P('seq', None, 'fsdp')
- grad_out: float32 [1024, 1024], P('fsdp', 'seq')
- grad_in: float32 [1024, 2, 2624], P('seq', None, 'fsdp')
- grad_down: float32 [2624, 1024], P('fsdp', 'seq')
- grad_gain_attn: float32 [1024], P('fsdp')
- grad_gain_mlp: float32 [1024], P('fsdp')
The draws below stay inside these ranges and needn't reach their ends.
Inputs may be any that keep to these rules, and one draw needn't show every extreme that they name: `doc_ids`: never falling along a group; each number is one contiguous document; one document of a group holds 512 tokens.
All inputs are finite; a program needn't handle non-finite values.
Results may differ from the reference program's by a relative error of at most 0.018.
Values may be sent and summed in bfloat16 or wider, within the bound.
No kernel may reach another device: no remote copies, remote signals or barrier semaphores. Data moves between devices by JAX's collectives and lax.ppermute only.
A program may use at most 128 MiB of HBM per device.

```python
import math
import jax
import jax.numpy as jnp
import numpy as np
from jax import lax

D = 1024
HEADS = 16
HD = 64
FF = 2624
HALO = 64
DOCS = 4
TOK_DEV = 128
HH = 1024
ROWS = 1024
GROUPS = 4


def draw_w_qkv(key, part):
    head_cols = HEADS * HD
    entries = jax.random.truncated_normal(key, -4.0, 4.0, (D, 3, head_cols), jnp.float32) / math.sqrt(D)
    return entries.astype(jnp.bfloat16)


def block_scale(key, shape, pieces, low, high):
    gain, own = 1.0, jax.random.fold_in(key, 6)
    for position, parts in pieces:
        heights = jnp.exp(jax.random.uniform(jax.random.fold_in(own, position), (parts,), jnp.float32, low / len(pieces), high / len(pieces)))
        gain = gain * jnp.repeat(heights, shape[position] // parts).reshape([-1 if axis == position else 1 for axis in range(len(shape))])
    return gain


def profile(count, total, reach, slope):
    portions = [(1 << 20) // math.isqrt(grade ** slope) + 1 for grade in range(2, count + 1)]
    surplus, counts = total - reach - (count - 1), [1] * (count - 1)
    while surplus > 0:
        free = [i for i in range(count - 1) if counts[i] < reach]
        mass, budget = sum([portions[i] for i in free]), surplus
        for i in free:
            more = min(reach - counts[i], max(1, budget * portions[i] // mass), surplus)
            counts[i] = counts[i] + more
            surplus = surplus - more
    return np.array([reach] + counts)


def ragged_sizes(stream_key, amount, total, limit, slope):
    if amount == 2:
        one = jax.random.randint(stream_key, (), max(1, total - limit), min(limit, total - 1) + 1)
        return jnp.stack([one, total - one])
    tallies = jnp.asarray(profile(amount, total, limit, slope), jnp.int32)
    couples = (amount - 1) // 2
    giver, receiver = tallies[1:1 + 2 * couples:2], tallies[2:2 + 2 * couples:2]
    room = jnp.minimum(giver - 1, limit - receiver)
    shifted = jax.random.randint(jax.random.fold_in(stream_key, 1), (couples,), 0, 1 << 20) % (room + 1)
    tallies = tallies.at[1:1 + 2 * couples:2].set(giver - shifted).at[2:2 + 2 * couples:2].set(receiver + shifted)
    return tallies[jax.random.permutation(jax.random.fold_in(stream_key, 2), amount)]


def noise(rng, extent, width, most, cuts=(), held_as=jnp.bfloat16):
    gain = block_scale(rng, extent, cuts, -0.22, 0.18) if cuts else 1.0
    values = jax.random.normal(rng, extent, jnp.float32) * width * gain
    return jnp.minimum(jnp.maximum(values, -most), most).astype(held_as)


def setup_inputs(seed: int = 0) -> dict:
    splits = jax.random.split(jax.random.key(seed), 10)
    block_input = noise(splits[0], (GROUPS, ROWS, D), 1.0, 6.0, ((0, 4), (1, 8)))
    doc_ids = jax.vmap(lambda own: jnp.searchsorted(jnp.cumsum(ragged_sizes(own, DOCS, ROWS, ROWS // 2, 0)), jnp.arange(ROWS), side="right"))(jax.random.split(splits[1], GROUPS)).reshape((GROUPS, ROWS)).astype(jnp.int32)
    gain_attn = jnp.clip(1.0 + 0.1 * jax.random.normal(splits[2], (D,), jnp.float32), 0.5, 1.5).astype(jnp.bfloat16)
    gain_mlp = jnp.clip(1.0 + 0.1 * jax.random.normal(splits[3], (D,), jnp.float32), 0.5, 1.5).astype(jnp.bfloat16)
    w_qkv = draw_w_qkv(jax.random.fold_in(splits[9], 71), 0)
    w_out = noise(splits[5], (HH, D), (HH // 64) ** -0.5, 1.5, ((0, 4),))
    w_in = noise(splits[6], (D, 2, FF), D ** -0.5, 0.1875, ((2, 4),))
    w_down = noise(splits[7], (FF, D), FF ** -0.5, 0.125, ((0, 4),))
    out_grad = noise(splits[8], (GROUPS, ROWS, D), 1.0, 6.0, ((0, 4), (1, 8)))
    return dict(block_input=block_input, doc_ids=doc_ids, gain_attn=gain_attn, gain_mlp=gain_mlp, w_qkv=w_qkv, w_out=w_out, w_in=w_in, w_down=w_down, out_grad=out_grad)


EPSILON = 1e-05
THETA = 10000.0

def norm_rows(values, gain_row):
    center = values - lax.optimization_barrier(jnp.mean(values, axis=-1, keepdims=True))
    spread = lax.optimization_barrier(jnp.mean(center * center, axis=-1, keepdims=True))
    return center * lax.rsqrt(spread + EPSILON) * gain_row

def rotary_tables(positions):
    half_dim = HD // 2
    inverse = THETA ** (-(jnp.arange(half_dim, dtype=jnp.float32) * 2.0 / HD))
    phases = positions.astype(jnp.float32)[:, None] * inverse[None, :]
    cosine_half = jnp.cos(phases)
    sine_half = jnp.sin(phases)
    return (jnp.concatenate([cosine_half, cosine_half], -1), jnp.concatenate([sine_half, sine_half], -1))

def rotate(values, cosine_table, sine_table):
    half_dim = HD // 2
    turned = jnp.concatenate([-values[..., half_dim:], values[..., :half_dim]], -1)
    return values * cosine_table[:, None, :] + turned * sine_table[:, None, :]

def rotate_back(upstream, cosine_table, sine_table):
    half_dim = HD // 2
    scaled = upstream * sine_table[:, None, :]
    turned = jnp.concatenate([scaled[..., half_dim:], -scaled[..., :half_dim]], -1)
    return upstream * cosine_table[:, None, :] + turned

def gated_unit(inner_in, inner_gate):
    return jax.nn.gelu(inner_in, approximate=False) * inner_gate

def window_mask(ids_query, ids_key):
    query_pos = jnp.arange(ids_query.shape[0], dtype=jnp.int32)[:, None]
    key_pos = jnp.arange(ids_key.shape[0], dtype=jnp.int32)[None, :] - HALO
    return (jnp.abs(query_pos - key_pos) <= HALO) & (ids_query[:, None] == ids_key[None, :])

def split_heads(values):
    return values.reshape(values.shape[0], HEADS, HD)

def product(form, left_op, right_op):
    return jnp.einsum(form, left_op.astype(jnp.float32), right_op.astype(jnp.float32))

def attention_scores(queries, keyvals, ids_query, ids_key):
    head_cols = HEADS * HD
    logits = product('qhd,khd->hqk', split_heads(queries), split_heads(keyvals[:, :head_cols])) * HD ** (-0.5)
    return jnp.where(window_mask(ids_query, ids_key)[None], logits, -jnp.inf)

def attend(queries, keyvals, ids_query, ids_key):
    head_cols = HEADS * HD
    logits = attention_scores(queries, keyvals, ids_query, ids_key)
    highest = lax.optimization_barrier(jnp.max(logits, axis=-1))
    logsum = highest + jnp.log(lax.optimization_barrier(jnp.sum(jnp.exp(logits - highest[..., None]), axis=-1)))
    weights = jnp.exp(logits - logsum[..., None]).astype(jnp.bfloat16)
    combined = product('hqk,khd->qhd', weights, split_heads(keyvals[:, head_cols:]))
    return (combined.reshape(queries.shape[0], head_cols).astype(jnp.bfloat16), logsum)

def attend_back(queries, keyvals, ids_query, ids_key, attended, logsum, d_attended):
    head_cols = HEADS * HD
    logits = attention_scores(queries, keyvals, ids_query, ids_key)
    probability = jnp.exp(logits - logsum[..., None])
    weights = probability.astype(jnp.bfloat16)
    d_heads = split_heads(d_attended)
    value_heads = split_heads(keyvals[:, head_cols:])
    d_values = product('hqk,qhd->khd', weights, d_heads)
    d_probs = product('qhd,khd->hqk', d_heads, value_heads)
    row_dots = lax.optimization_barrier(jnp.sum(d_heads.astype(jnp.float32) * split_heads(attended).astype(jnp.float32), axis=-1)).T
    d_logits = (probability * (d_probs - row_dots[..., None]) * HD ** (-0.5)).astype(jnp.bfloat16)
    d_query_heads = product('hqk,khd->qhd', d_logits, split_heads(keyvals[:, :head_cols]))
    d_key_heads = product('hqk,qhd->khd', d_logits, split_heads(queries))
    key_count = keyvals.shape[0]
    d_window = jnp.concatenate([d_key_heads.reshape(key_count, head_cols), d_values.reshape(key_count, head_cols)], axis=1)
    return (d_query_heads.reshape(queries.shape[0], head_cols), d_window)

def reference(block_input, doc_ids, gain_attn, gain_mlp, w_qkv, w_out, w_in, w_down, out_grad):
    head_cols = HEADS * HD
    flat_qkv = w_qkv.reshape(D, 3 * head_cols)
    flat_in = w_in.reshape(D, 2 * FF)
    gain_one = gain_attn.astype(jnp.float32)
    gain_two = gain_mlp.astype(jnp.float32)
    cosine_table, sine_table = rotary_tables(jnp.arange(ROWS, dtype=jnp.int32))
    starts = jnp.arange(ROWS // TOK_DEV, dtype=jnp.int32) * TOK_DEV
    window = TOK_DEV + 2 * HALO

    def one_group(totals, group_data):
        tokens, ids_all, upstream = group_data
        inputs = tokens.astype(jnp.float32)
        normed = norm_rows(inputs, gain_one).astype(jnp.bfloat16)
        projected = jnp.dot(normed, flat_qkv, preferred_element_type=jnp.float32)
        queries = rotate(split_heads(projected[:, :head_cols]), cosine_table, sine_table).reshape(ROWS, head_cols).astype(jnp.bfloat16)
        key_rows = rotate(split_heads(projected[:, head_cols:2 * head_cols]), cosine_table, sine_table).reshape(ROWS, head_cols)
        keyvals = jnp.concatenate([key_rows, projected[:, 2 * head_cols:]], axis=1).astype(jnp.bfloat16)
        padded_kv = jnp.pad(keyvals, ((HALO, HALO), (0, 0)))
        padded_ids = jnp.pad(ids_all, (HALO, HALO), constant_values=-1)

        def forward_block(offset):
            return attend(lax.dynamic_slice_in_dim(queries, offset, TOK_DEV, 0), lax.dynamic_slice_in_dim(padded_kv, offset, window, 0), lax.dynamic_slice_in_dim(ids_all, offset, TOK_DEV, 0), lax.dynamic_slice_in_dim(padded_ids, offset, window, 0))
        attended, logsum = lax.map(forward_block, starts)
        attended = attended.reshape(ROWS, head_cols)
        after_attn = inputs + jnp.dot(attended, w_out, preferred_element_type=jnp.float32)
        normed_two = norm_rows(after_attn, gain_two).astype(jnp.bfloat16)
        lifted = jnp.dot(normed_two, flat_in, preferred_element_type=jnp.float32)
        activated, act_back = jax.vjp(gated_unit, lifted[:, :FF], lifted[:, FF:])
        activated = activated.astype(jnp.bfloat16)
        result = after_attn + jnp.dot(activated, w_down, preferred_element_type=jnp.float32)
        grad_down = jnp.dot(activated.T, upstream, preferred_element_type=jnp.float32)
        d_active = jnp.dot(upstream, w_down.T, preferred_element_type=jnp.float32)
        d_inner, d_gate = act_back(d_active)
        d_lifted = jnp.concatenate([d_inner, d_gate], axis=1).astype(jnp.bfloat16)
        grad_in = jnp.dot(normed_two.T, d_lifted, preferred_element_type=jnp.float32)
        d_normed_two = jnp.dot(d_lifted, flat_in.T, preferred_element_type=jnp.float32)
        d_after_norm, grad_gain_two = jax.vjp(norm_rows, after_attn, gain_two)[1](d_normed_two)
        d_after = upstream.astype(jnp.float32) + d_after_norm
        d_after_half = d_after.astype(jnp.bfloat16)
        grad_out = jnp.dot(attended.T, d_after_half, preferred_element_type=jnp.float32)
        d_attended = jnp.dot(d_after_half, w_out.T, preferred_element_type=jnp.float32).astype(jnp.bfloat16)

        def backward_block(offset):
            block_index = offset // TOK_DEV
            return attend_back(lax.dynamic_slice_in_dim(queries, offset, TOK_DEV, 0), lax.dynamic_slice_in_dim(padded_kv, offset, window, 0), lax.dynamic_slice_in_dim(ids_all, offset, TOK_DEV, 0), lax.dynamic_slice_in_dim(padded_ids, offset, window, 0), lax.dynamic_slice_in_dim(attended, offset, TOK_DEV, 0), logsum[block_index], lax.dynamic_slice_in_dim(d_attended, offset, TOK_DEV, 0))
        d_queries, d_window = lax.map(backward_block, starts)
        own_rows = d_window[:, HALO:HALO + TOK_DEV]
        own_rows = own_rows.at[:-1, TOK_DEV - HALO:].add(d_window[1:, :HALO])
        own_rows = own_rows.at[1:, :HALO].add(d_window[:-1, HALO + TOK_DEV:])
        d_keyvals = own_rows.reshape(ROWS, 2 * head_cols)
        d_queries = d_queries.reshape(ROWS, head_cols)
        d_qkv = jnp.concatenate([rotate_back(split_heads(d_queries), cosine_table, sine_table).reshape(ROWS, head_cols), rotate_back(split_heads(d_keyvals[:, :head_cols]), cosine_table, sine_table).reshape(ROWS, head_cols), d_keyvals[:, head_cols:]], axis=1).astype(jnp.bfloat16)
        grad_qkv = jnp.dot(normed.T, d_qkv, preferred_element_type=jnp.float32)
        d_normed = jnp.dot(d_qkv, flat_qkv.T, preferred_element_type=jnp.float32)
        d_inputs, grad_gain_one = jax.vjp(norm_rows, inputs, gain_one)[1](d_normed)
        d_tokens = d_after + d_inputs
        partials = (grad_qkv, grad_out, grad_in, grad_down, grad_gain_one, grad_gain_two)
        totals = jax.tree.map(jnp.add, totals, partials)
        return (totals, (result.astype(jnp.bfloat16), d_tokens))
    initial = (jnp.zeros((D, 3 * head_cols), jnp.float32), jnp.zeros((head_cols, D), jnp.float32), jnp.zeros((D, 2 * FF), jnp.float32), jnp.zeros((FF, D), jnp.float32), jnp.zeros((D,), jnp.float32), jnp.zeros((D,), jnp.float32))
    totals, outputs = lax.scan(one_group, initial, (block_input, doc_ids, out_grad))
    return (outputs[0], outputs[1], totals[0].reshape(D, 3, head_cols), totals[1], totals[2].reshape(D, 2, FF), totals[3], totals[4], totals[5])
```

```python
import functools

import jax
import jax.numpy as jnp
from jax import lax
from jax.experimental import pallas as pl
from jax.experimental.pallas import tpu as pltpu
from jax.sharding import PartitionSpec as P

HD = 64
HALO = 64
EPSILON = 1e-05
THETA = 10000.0
LANES = 128
MASKED = -1e30
HALF = jnp.bfloat16
FULL = jnp.float32


def dot_nn(a, b):
    return lax.dot_general(a, b, (((1,), (0,)), ((), ())), preferred_element_type=FULL)


def dot_nt(a, b):
    return lax.dot_general(a, b, (((1,), (1,)), ((), ())), preferred_element_type=FULL)


def dot_tn(a, b):
    return lax.dot_general(a, b, (((0,), (0,)), ((), ())), preferred_element_type=FULL)


def shape(dims, dtype):
    return jax.ShapeDtypeStruct(tuple(dims), dtype)


def call(kernel, outs, *args, scalars=0, flops=0, name=None):
    smem = pl.BlockSpec(memory_space=pltpu.SMEM)
    vmem = pl.BlockSpec(memory_space=pltpu.VMEM)
    moved = sum(a.size * a.dtype.itemsize for a in args)
    moved += sum(o.size * o.dtype.itemsize for o in outs)
    return pl.pallas_call(
        kernel,
        out_shape=tuple(outs),
        in_specs=[smem] * scalars + [vmem] * (len(args) - scalars),
        out_specs=tuple([vmem] * len(outs)),
        cost_estimate=pl.CostEstimate(flops=flops, transcendentals=0, bytes_accessed=moved),
        compiler_params=pltpu.CompilerParams(vmem_limit_bytes=60 << 20),
        name=name,
    )(*args)


def norm_parts(z):
    center = z - jnp.mean(z, axis=-1, keepdims=True)
    scale = lax.rsqrt(jnp.mean(center * center, axis=-1, keepdims=True) + EPSILON)
    return center * scale, scale


def norm_back(z, gain, upstream):
    zhat, scale = norm_parts(z)
    f = upstream * gain
    inner = f - jnp.mean(f, axis=-1, keepdims=True)
    inner = inner - zhat * jnp.mean(f * zhat, axis=-1, keepdims=True)
    return scale * inner, zhat


def swap_halves(u):
    lane = lax.broadcasted_iota(jnp.int32, (1, LANES), 1)
    first = (lane % HD) < (HD // 2)
    return jnp.where(
        first, pltpu.roll(u, LANES - HD // 2, 1), pltpu.roll(u, HD // 2, 1)
    )


def head_masks():
    lane = lax.broadcasted_iota(jnp.int32, (1, LANES), 1)
    low = lane < HD
    return low, (low.astype(FULL).astype(HALF), (~low).astype(FULL).astype(HALF))


def stacked_mid(ref, tok, halo):
    ext = tok + 2 * halo
    return jnp.concatenate([ref[halo : halo + tok], ref[ext + halo : ext + halo + tok]], axis=0)


def attention_forward(normed_ref, w_ref, cos_ref, sin_ref, bias_ref, q_ref, k_ref, v_ref, att_ref, p_ref):
    tok, ext = bias_ref.shape[1:]
    halo = (ext - tok) // 2
    cols = w_ref.shape[2]
    pairs = cols // LANES
    normed = normed_ref[...]
    key_part = dot_nn(normed, w_ref[1])
    v_ref[...] = dot_nn(normed, w_ref[2]).astype(HALF)
    query_part = dot_nn(stacked_mid(normed_ref, tok, halo), w_ref[0]) * HD ** (-0.5)
    cos, sin = cos_ref[...], sin_ref[...]
    for g in range(2):
        for j in range(pairs):
            part = slice(j * LANES, (j + 1) * LANES)
            u = key_part[g * ext : (g + 1) * ext, part]
            k_ref[g * ext : (g + 1) * ext, part] = (u * cos + swap_halves(u) * sin).astype(HALF)
            u = query_part[g * tok : (g + 1) * tok, part]
            turned = u * cos[halo : halo + tok] + swap_halves(u) * sin[halo : halo + tok]
            q_ref[g * tok : (g + 1) * tok, part] = turned.astype(HALF)
    low, masks = head_masks()
    for g in range(2):
        bias = bias_ref[g]
        for j in range(pairs):
            part = slice(j * LANES, (j + 1) * LANES)
            q = q_ref[g * tok : (g + 1) * tok, part]
            k = k_ref[g * ext : (g + 1) * ext, part]
            v = v_ref[g * ext : (g + 1) * ext, part]
            found = []
            for h in range(2):
                s = dot_nt(q * masks[h], k) + bias
                e = jnp.exp(s - jnp.max(s, axis=-1, keepdims=True))
                p = (e * (1.0 / jnp.sum(e, axis=-1, keepdims=True))).astype(HALF)
                p_ref[(g * pairs + j) * 2 + h] = p
                found.append(dot_nn(p, v))
            att_ref[g * tok : (g + 1) * tok, part] = jnp.where(low, found[0], found[1]).astype(HALF)


def split_store(core, value, keep, send, m, rows):
    a, b = value(0), value(1)
    even = core == 0
    keep[m, rows] = jnp.where(even, a, b).astype(HALF)
    send[m, rows] = jnp.where(even, b, a).astype(HALF)


def attention_backward(
    core, normed_ref, w_ref, wo_ref, cos_ref, sin_ref, q_ref, k_ref, v_ref, att_ref, p_ref, da, dn_ref, keep, send
):
    tok, ext = p_ref.shape[1:]
    halo = (ext - tok) // 2
    cols = w_ref.shape[2]
    pairs = cols // LANES
    width = wo_ref.shape[1]
    blocks = width // (2 * LANES)
    d_att = dot_nt(da, wo_ref[...]).astype(HALF)
    cos, sin = cos_ref[...], sin_ref[...]
    mid_cos, mid_sin = cos[halo : halo + tok], sin[halo : halo + tok]
    low, masks = head_masks()
    all_dq, all_dk, all_dv = [], [], []
    for g in range(2):
        row_dq, row_dk, row_dv = [], [], []
        for j in range(pairs):
            part = slice(j * LANES, (j + 1) * LANES)
            q = q_ref[g * tok : (g + 1) * tok, part]
            k = k_ref[g * ext : (g + 1) * ext, part]
            v = v_ref[g * ext : (g + 1) * ext, part]
            do = d_att[g * tok : (g + 1) * tok, part]
            att = att_ref[g * tok : (g + 1) * tok, part]
            both = do.astype(FULL) * att.astype(FULL)
            dq, dk, dv = [], [], []
            for h in range(2):
                p = p_ref[(g * pairs + j) * 2 + h]
                dp = dot_nt(do * masks[h], v)
                dots = jnp.sum(jnp.where(low if h == 0 else ~low, both, 0.0), axis=-1, keepdims=True)
                ds = (p.astype(FULL) * (dp - dots)).astype(HALF)
                dq.append(dot_nn(ds, k))
                dk.append(dot_tn(ds, q))
                dv.append(dot_tn(p, do))
            u = jnp.where(low, dq[0], dq[1]) * HD ** (-0.5)
            row_dq.append((u * mid_cos - swap_halves(u) * mid_sin).astype(HALF))
            u = jnp.where(low, dk[0], dk[1])
            row_dk.append((u * cos - swap_halves(u) * sin).astype(HALF))
            row_dv.append(jnp.where(low, dv[0], dv[1]).astype(HALF))
        all_dq.append(jnp.concatenate(row_dq, axis=1))
        all_dk.append(jnp.concatenate(row_dk, axis=1))
        all_dv.append(jnp.concatenate(row_dv, axis=1))
    dq = jnp.concatenate(all_dq, axis=0)
    dk = jnp.concatenate(all_dk, axis=0)
    dv = jnp.concatenate(all_dv, axis=0)
    normed = normed_ref[...]
    mid = stacked_mid(normed_ref, tok, halo)
    for c, (left, right) in enumerate(((mid, dq), (normed, dk), (normed, dv))):
        grad = dot_tn(left, right)
        for m in range(blocks):
            for j in range(pairs):
                rows = slice((c * pairs + j) * LANES, (c * pairs + j + 1) * LANES)
                split_store(
                    core,
                    lambda i: grad[(2 * m + i) * LANES : (2 * m + i + 1) * LANES, j * LANES : (j + 1) * LANES],
                    keep, send, m, rows,
                )
    grad = dot_tn(att_ref[...], da)
    rows = slice(3 * cols, 4 * cols)
    for m in range(blocks):
        split_store(
            core, lambda i: grad[:, (2 * m + i) * LANES : (2 * m + i + 1) * LANES], keep, send, m, rows
        )
    d_mid = dot_nt(dq, w_ref[0])
    d_all = dot_nt(dk, w_ref[1]) + dot_nt(dv, w_ref[2])
    for g in range(2):
        base = g * ext
        dn_ref[base : base + halo] = d_all[base : base + halo]
        dn_ref[base + halo : base + halo + tok] = (
            d_all[base + halo : base + halo + tok] + d_mid[g * tok : (g + 1) * tok]
        )
        dn_ref[base + halo + tok : base + ext] = d_all[base + halo + tok : base + ext]


def first_kernel(
    mid_ref, bef_ref, aft_ref, pmid_ref, pbef_ref, paft_ref, gain_ref, w_ref, wo_ref, cos_ref, sin_ref, bias_ref,
    normed_ref, q_ref, k_ref, v_ref, att_ref, p_ref, part_ref,
):
    gain = gain_ref[...].astype(FULL)
    row = 0
    for ref in (bef_ref, mid_ref, aft_ref, pbef_ref, pmid_ref, paft_ref):
        zhat, _ = norm_parts(ref[...].astype(FULL))
        normed_ref[row : row + ref.shape[0]] = (zhat * gain).astype(HALF)
        row += ref.shape[0]
    attention_forward(normed_ref, w_ref, cos_ref, sin_ref, bias_ref, q_ref, k_ref, v_ref, att_ref, p_ref)
    part_ref[...] = dot_nn(att_ref[...], wo_ref[...])


def unpack_first(scalar_ref, sources, w_ref, wo_ref):
    cols = w_ref.shape[2]
    pairs = cols // LANES
    for i, (block, read) in enumerate(sources):
        at = pl.ds(pl.multiple_of(block * LANES, LANES), LANES)
        for c in range(3):
            for j in range(pairs):
                start = (c * pairs + j) * LANES
                w_ref[c, at, j * LANES : (j + 1) * LANES] = read(slice(start, start + LANES))
        wo_ref[:, at] = read(slice(3 * cols, 4 * cols))


def second_kernel(count, scalar_ref, normed_ref, *refs):
    own = refs[:count]
    other_ref = refs[count]
    cos_ref, sin_ref, bias_ref, part_ref = refs[count + 1 : count + 5]
    w_ref, wo_ref, q_ref, k_ref, v_ref, att_ref, p_ref, send_ref, keep_ref = refs[count + 5 :]
    place, core = scalar_ref[0], scalar_ref[1]
    sources = []
    for i in range(count):
        sources.append(((place ^ i) * 2 + core, lambda rows, i=i: own[i][rows]))
        sources.append(((place ^ i) * 2 + 1 - core, lambda rows, i=i: other_ref[i, rows]))
    unpack_first(scalar_ref, sources, w_ref, wo_ref)
    second_tail(normed_ref, w_ref, wo_ref, cos_ref, sin_ref, bias_ref, part_ref, q_ref, k_ref, v_ref, att_ref, p_ref, send_ref, keep_ref)


def second_whole_kernel(
    normed_ref, w_ref, wo_ref, cos_ref, sin_ref, bias_ref, part_ref, q_ref, k_ref, v_ref, att_ref, p_ref, send_ref, keep_ref
):
    second_tail(normed_ref, w_ref, wo_ref, cos_ref, sin_ref, bias_ref, part_ref, q_ref, k_ref, v_ref, att_ref, p_ref, send_ref, keep_ref)


def second_tail(
    normed_ref, w_ref, wo_ref, cos_ref, sin_ref, bias_ref, part_ref, q_ref, k_ref, v_ref, att_ref, p_ref, send_ref, keep_ref
):
    attention_forward(normed_ref, w_ref, cos_ref, sin_ref, bias_ref, q_ref, k_ref, v_ref, att_ref, p_ref)
    tok = keep_ref.shape[0]
    total = part_ref[...] + dot_nn(att_ref[...], wo_ref[...])
    keep_ref[...] = total[:tok]
    send_ref[...] = total[tok:].astype(HALF)


def middle_kernel(x_ref, keep_ref, recv_ref, gain_ref, after_ref, normed_ref):
    after = x_ref[...].astype(FULL) + (keep_ref[...] + recv_ref[...].astype(FULL))
    after_ref[...] = after
    zhat, _ = norm_parts(after)
    normed_ref[...] = (zhat * gain_ref[...].astype(FULL)).astype(HALF)


def gate_kernel(
    x_ref, px_ref, og_ref, pog_ref, win_ref, wdown_ref, win_far_ref, wdown_far_ref, act_ref, dl_ref, send_ref, keep_ref
):
    tok = x_ref.shape[0]
    x = jnp.concatenate([x_ref[...], px_ref[...]], axis=0)
    og = jnp.concatenate([og_ref[...], pog_ref[...]], axis=0)
    total = None
    for n, (win, wdown) in enumerate(((win_ref, wdown_ref), (win_far_ref, wdown_far_ref))):
        a = dot_nt(x, win[0])
        b = dot_nt(x, win[1])
        d_act = dot_nt(og, wdown[...])
        phi = 0.5 * (1.0 + lax.erf(a * 0.7071067811865476))
        density = jnp.exp(-0.5 * a * a) * 0.3989422804014327
        gelu = a * phi
        act_ref[n] = (gelu * b).astype(HALF)
        da = (d_act * b * (phi + a * density)).astype(HALF)
        db = (d_act * gelu).astype(HALF)
        dl_ref[n, 0] = da
        dl_ref[n, 1] = db
        part = dot_nn(da, win[0]) + dot_nn(db, win[1])
        total = part if total is None else total + part
    keep_ref[...] = total[:tok]
    send_ref[...] = total[tok:].astype(HALF)


def result_kernel(act_ref, wdown_ref, wdown_far_ref, send_ref, keep_ref):
    tok = keep_ref.shape[0]
    total = dot_nn(act_ref[0], wdown_ref[...]) + dot_nn(act_ref[1], wdown_far_ref[...])
    keep_ref[...] = total[:tok]
    send_ref[...] = total[tok:].astype(HALF)


def gate_grad_kernel(n, scalar_ref, x_ref, px_ref, og_ref, pog_ref, act_ref, dl_ref, keep_ref, send_ref):
    core = scalar_ref[1]
    hidden = act_ref.shape[2]
    blocks = x_ref.shape[1] // (2 * LANES)
    x = jnp.concatenate([x_ref[...], px_ref[...]], axis=0)
    og = jnp.concatenate([og_ref[...], pog_ref[...]], axis=0)
    for c, (left, right) in enumerate(((dl_ref[n, 0], x), (dl_ref[n, 1], x), (act_ref[n], og))):
        grad = dot_tn(left, right)
        rows = slice(c * hidden, (c + 1) * hidden)
        for m in range(blocks):
            split_store(
                core, lambda i: grad[:, (2 * m + i) * LANES : (2 * m + i + 1) * LANES], keep_ref, send_ref, m, rows
            )


def middle_back_kernel(after_ref, gain_ref, keep_ref, recv_ref, og_ref, da_ref, half_ref, gsum_ref):
    upstream = keep_ref[...] + recv_ref[...].astype(FULL)
    d_norm, zhat = norm_back(after_ref[...], gain_ref[...].astype(FULL), upstream)
    gsum_ref[...] = jnp.sum(upstream * zhat, axis=0, keepdims=True)
    d_after = og_ref[...].astype(FULL) + d_norm
    da_ref[...] = d_after
    half_ref[...] = d_after.astype(HALF)


def far_back_kernel(
    scalar_ref, normed_ref, w_ref, wo_ref, cos_ref, sin_ref, q_ref, k_ref, v_ref, att_ref, p_ref, da_ref, pda_ref,
    keep, send, dn_ref,
):
    da = jnp.concatenate([da_ref[...], pda_ref[...]], axis=0)
    attention_backward(
        scalar_ref[1], normed_ref, w_ref, wo_ref, cos_ref, sin_ref, q_ref, k_ref, v_ref, att_ref, p_ref, da, dn_ref,
        keep, send,
    )


def own_back_kernel(
    scalar_ref, normed_ref, w_ref, wo_ref, cos_ref, sin_ref, q_ref, k_ref, v_ref, att_ref, p_ref, da_ref, pda_ref,
    far_ref, gain_ref, keep, send, mid_ref, pmid_ref, bef_ref, aft_ref, pbef_ref, paft_ref, gsum_ref, dn_ref,
):
    tok, ext = p_ref.shape[1:]
    halo = (ext - tok) // 2
    da = jnp.concatenate([da_ref[...], pda_ref[...]], axis=0)
    attention_backward(
        scalar_ref[1], normed_ref, w_ref, wo_ref, cos_ref, sin_ref, q_ref, k_ref, v_ref, att_ref, p_ref, da, dn_ref,
        keep, send,
    )
    total = dn_ref[...] + far_ref[...]
    gsum_ref[...] = jnp.sum(total * normed_ref[...].astype(FULL), axis=0, keepdims=True) / gain_ref[...].astype(FULL)
    mid_ref[...] = total[halo : halo + tok]
    bef_ref[...] = total[:halo].astype(HALF)
    aft_ref[...] = total[halo + tok : ext].astype(HALF)
    pmid_ref[...] = total[ext + halo : ext + halo + tok].astype(HALF)
    pbef_ref[...] = total[ext : ext + halo].astype(HALF)
    paft_ref[...] = total[ext + halo + tok :].astype(HALF)


def last_kernel(x_ref, gain_ref, da_ref, keep_ref, pair_ref, f0_ref, f1_ref, l0_ref, l1_ref, out_ref):
    tok, halo = keep_ref.shape[0], f0_ref.shape[0]
    total = keep_ref[...] + pair_ref[...].astype(FULL)
    first = f0_ref[...].astype(FULL) + f1_ref[...].astype(FULL)
    last = l0_ref[...].astype(FULL) + l1_ref[...].astype(FULL)
    pieces = [total[:halo] + first]
    if tok > 2 * halo:
        pieces.append(total[halo : tok - halo])
    pieces.append(total[tok - halo :] + last)
    total = jnp.concatenate(pieces, axis=0)
    d_norm, _ = norm_back(x_ref[...].astype(FULL), gain_ref[...].astype(FULL), total)
    out_ref[...] = da_ref[...] + d_norm


def share_kernel(scalar_ref, keep_ref, recv_ref, own_ref, *sends):
    place = scalar_ref[0]
    own_ref[...] = keep_ref[place].astype(FULL) + recv_ref[place].astype(FULL)
    for i, out in enumerate(sends):
        at = place ^ (i + 1)
        out[...] = (keep_ref[at].astype(FULL) + recv_ref[at].astype(FULL)).astype(HALF)


def total_kernel(count, own_ref, *refs):
    total = own_ref[...]
    for r in refs[:count]:
        total = total + r[...].astype(FULL)
    out = refs[count]
    out[...] = total.astype(out.dtype)


def pack_first_kernel(scalar_ref, w_ref, wo_ref, out_ref):
    pairs = w_ref.shape[2] // LANES
    for c in range(3):
        for j in range(pairs):
            start = (c * pairs + j) * LANES
            out_ref[start : start + LANES] = w_ref[c, :, j * LANES : (j + 1) * LANES]
    out_ref[3 * pairs * LANES :] = wo_ref[...]


def pack_gate_kernel(scalar_ref, win_ref, wdown_ref, out_ref):
    hidden = wdown_ref.shape[0]
    out_ref[:hidden] = win_ref[0]
    out_ref[hidden : 2 * hidden] = win_ref[1]
    out_ref[2 * hidden :] = wdown_ref[...]


def pack(kernel, scalars, left, left_block, right, right_block, rows):
    return pl.pallas_call(
        kernel,
        grid_spec=pltpu.PrefetchScalarGridSpec(
            num_scalar_prefetch=1,
            grid=(1,),
            in_specs=[pl.BlockSpec(*left_block), pl.BlockSpec(*right_block)],
            out_specs=pl.BlockSpec((rows, LANES), lambda i, s: (0, 0)),
        ),
        out_shape=shape((rows, LANES), HALF),
    )(scalars, left, right)


def exchange(value, axis, bit):
    return lax.ppermute(value, axis, [(i, i ^ bit) for i in range(lax.axis_size(axis))])


def move(value, step, bit):
    seq, fsdp = lax.axis_size("seq"), lax.axis_size("fsdp")
    pairs = [
        (s * fsdp + f, (s + step) * fsdp + (f ^ bit))
        for s in range(seq)
        if 0 <= s + step < seq
        for f in range(fsdp)
    ]
    return lax.ppermute(value, ("seq", "fsdp"), pairs)


def seq_totals(scalars, keep, send):
    seq = lax.axis_size("seq")
    half, rows = keep.shape[:2]
    if 2 * half == seq:
        recv = exchange(send, "seq", 1)
        outs = call(
            share_kernel, [shape((rows, LANES), FULL)] + [shape((rows, LANES), HALF)] * (half - 1),
            scalars, keep, recv, scalars=1, name="share",
        )
        got = [exchange(v, "seq", 2 * (i + 1)) for i, v in enumerate(outs[1:])]
        return outs[0], got
    return None


def whole_blocks(scalars, keep, send):
    even = scalars[1] == 0
    pair = jnp.stack([jnp.where(even, keep, send), jnp.where(even, send, keep)], axis=1)
    return pair.reshape((2 * keep.shape[0],) + keep.shape[1:])


def add_all(own, got, dtype):
    return call(
        functools.partial(total_kernel, len(got)), [shape(own.shape, dtype)], own, *got, name="total"
    )[0]


def body(block_input, doc_ids, gain_attn, gain_mlp, w_qkv, w_out, w_in, w_down, out_grad):
    tok, width = block_input.shape[1:]
    cols = w_qkv.shape[2]
    hidden = w_in.shape[2]
    ext = tok + 2 * HALO
    seq, fsdp = lax.axis_size("seq"), lax.axis_size("fsdp")
    assert fsdp == 4 and width % (2 * LANES) == 0 and cols % LANES == 0
    blocked = width == seq * LANES
    place = lax.axis_index("seq")
    column = lax.axis_index("fsdp")
    scalars = jnp.stack([place // 2, place % 2, place]).astype(jnp.int32)
    x, og = block_input[0], out_grad[0]
    gain_one, gain_two = gain_attn[None], gain_mlp[None]
    own_qkv = jnp.transpose(w_qkv, (1, 0, 2))
    own_in = jnp.transpose(w_in, (1, 2, 0))

    if blocked:
        packed = pack(
            pack_first_kernel, scalars[2:], own_qkv, ((3, LANES, cols), lambda i, s: (0, s[0], 0)),
            w_out, ((cols, LANES), lambda i, s: (0, s[0])), 4 * cols,
        )
        packed = exchange(packed, "fsdp", 2)
    else:
        far_qkv, far_out = exchange(own_qkv, "fsdp", 2), exchange(w_out, "fsdp", 2)

    pair_x = exchange(x, "fsdp", 1)
    last_rows, first_rows = x[tok - HALO :], x[:HALO]
    before, after_rows = move(last_rows, 1, 0), move(first_rows, -1, 0)
    pair_before, pair_after = move(last_rows, 1, 1), move(first_rows, -1, 1)
    pair_og = exchange(og, "fsdp", 1)

    first_row = place * tok
    positions = (first_row - HALO + jnp.arange(ext, dtype=jnp.int32)).astype(FULL)
    lane = jnp.arange(LANES, dtype=jnp.int32)
    inverse = THETA ** (-((lane % (HD // 2)).astype(FULL) * 2.0 / HD))
    phases = positions[:, None] * inverse[None, :]
    cos = jnp.cos(phases)
    sin = jnp.sin(phases) * jnp.where((lane % HD) < HD // 2, -1.0, 1.0)[None, :]
    padded = jnp.pad(doc_ids, ((0, 0), (HALO, HALO)), constant_values=-1)
    ids_key = lax.dynamic_slice_in_dim(padded, first_row, ext, 1)
    ids_query = ids_key[:, HALO : HALO + tok]
    near = jnp.abs(jnp.arange(tok)[:, None] - (jnp.arange(ext)[None, :] - HALO)) <= HALO

    def bias_of(g):
        q = lax.dynamic_index_in_dim(ids_query, g, 0, keepdims=False)
        k = lax.dynamic_index_in_dim(ids_key, g, 0, keepdims=False)
        return jnp.where(near & (q[:, None] == k[None, :]), 0.0, MASKED).astype(FULL)

    bias = jnp.stack([bias_of(column), bias_of(column ^ 1)])

    heads = 2 * (cols // HD)
    saved = [
        shape((2 * tok, cols), HALF), shape((2 * ext, cols), HALF), shape((2 * ext, cols), HALF),
        shape((2 * tok, cols), HALF), shape((heads, tok, ext), HALF),
    ]
    attn_flops = 2 * (2 * ext * width * 2 * cols + 2 * tok * width * 2 * cols)
    normed, q0, k0, v0, att0, p0, part = call(
        first_kernel, [shape((2 * ext, width), HALF)] + saved + [shape((2 * tok, width), FULL)],
        x, before, after_rows, pair_x, pair_before, pair_after, gain_one, own_qkv, w_out, cos, sin, bias,
        flops=attn_flops, name="first",
    )
    halves = [shape((tok, width), HALF), shape((tok, width), FULL)]
    if blocked:
        count = seq // 2
        mine = [packed] + [exchange(packed, "seq", 2 * i) for i in range(1, count)]
        other = exchange(jnp.stack(mine), "seq", 1)
        far_qkv, far_out, q1, k1, v1, att1, p1, send, keep = call(
            functools.partial(second_kernel, count),
            [shape(own_qkv.shape, HALF), shape(w_out.shape, HALF)] + saved + halves,
            scalars, normed, *mine, other, cos, sin, bias, part, scalars=1, flops=attn_flops, name="second",
        )
        packed = pack(
            pack_gate_kernel, scalars[2:], own_in, ((2, hidden, LANES), lambda i, s: (0, 0, s[0])),
            w_down, ((hidden, LANES), lambda i, s: (0, s[0])), 3 * hidden,
        )
        packed = exchange(packed, "fsdp", 2)
        spread = lax.all_gather(packed, "seq", axis=0, tiled=False)
        spread = jnp.transpose(spread, (1, 0, 2)).reshape(3 * hidden, width)
        far_in, far_down = spread[: 2 * hidden].reshape(2, hidden, width), spread[2 * hidden :]
    else:
        q1, k1, v1, att1, p1, send, keep = call(
            second_whole_kernel, saved + halves, normed, far_qkv, far_out, cos, sin, bias, part,
            flops=attn_flops, name="second",
        )
        far_in, far_down = exchange(own_in, "fsdp", 2), exchange(w_down, "fsdp", 2)

    recv = exchange(send, "fsdp", 1)
    after, normed_two = call(
        middle_kernel, [shape((tok, width), FULL), shape((tok, width), HALF)], x, keep, recv, gain_two, name="middle"
    )
    pair_two = exchange(normed_two, "fsdp", 1)

    act, d_lifted, send, keep = call(
        gate_kernel, [shape((2, 2 * tok, hidden), HALF), shape((2, 2, 2 * tok, hidden), HALF)] + halves,
        normed_two, pair_two, og, pair_og, own_in, w_down, far_in, far_down,
        flops=2 * 2 * 5 * 2 * tok * hidden * width, name="gate",
    )
    recv = exchange(send, "fsdp", 1)
    res_send, res_keep = call(
        result_kernel, halves, act, w_down, far_down, flops=2 * 2 * 2 * tok * hidden * width, name="result"
    )
    res_recv = exchange(res_send, "fsdp", 1)
    blocks = width // (2 * LANES)
    gate_rows, attn_rows = 3 * hidden, 4 * cols

    def gate_grads(n):
        return call(
            functools.partial(gate_grad_kernel, n), [shape((blocks, gate_rows, LANES), HALF)] * 2,
            scalars, normed_two, pair_two, og, pair_og, act, d_lifted,
            scalars=1, flops=2 * 3 * 2 * tok * hidden * width, name="gate_grad",
        )

    gate_parts = (gate_grads(1), gate_grads(0))
    if blocked:
        gate_far, gate_own = seq_totals(scalars, *gate_parts[0]), seq_totals(scalars, *gate_parts[1])
    d_after, d_half, gsum_two = call(
        middle_back_kernel, [shape((tok, width), FULL), shape((tok, width), HALF), shape((1, width), FULL)],
        after, gain_two, keep, recv, og, name="middle_back",
    )
    pair_d = exchange(d_half, "fsdp", 1)
    result = (after + res_keep + res_recv.astype(FULL)).astype(HALF)

    grad_shapes = [shape((blocks, attn_rows, LANES), HALF)] * 2
    back_flops = 2 * (6 * 2 * ext * width * cols + 2 * 2 * tok * width * cols)
    keep, send, far_dn = call(
        far_back_kernel, grad_shapes + [shape((2 * ext, width), FULL)],
        scalars, normed, far_qkv, far_out, cos, sin, q1, k1, v1, att1, p1, d_half, pair_d,
        scalars=1, flops=back_flops, name="far_back",
    )
    attn_far_parts = (keep, send)
    if blocked:
        attn_far = seq_totals(scalars, keep, send)
    edge = shape((HALO, width), HALF)
    keep, send, mid, pair_mid, bef, aft, pbef, paft, gsum_one, _ = call(
        own_back_kernel,
        grad_shapes
        + [shape((tok, width), FULL), shape((tok, width), HALF), edge, edge, edge, edge, shape((1, width), FULL)]
        + [shape((2 * ext, width), FULL)],
        scalars, normed, own_qkv, w_out, cos, sin, q0, k0, v0, att0, p0, d_half, pair_d, far_dn, gain_one,
        scalars=1, flops=back_flops, name="own_back",
    )
    pair_mid = exchange(pair_mid, "fsdp", 1)
    last_own, last_pair = move(bef, -1, 0), move(pbef, -1, 1)
    first_own, first_pair = move(aft, 1, 0), move(paft, 1, 1)
    attn_own_parts = (keep, send)
    if blocked:
        attn_own = seq_totals(scalars, keep, send)
    grad_input = call(
        last_kernel, [shape((tok, width), FULL)],
        x, gain_one, d_after, mid, pair_mid, first_own, first_pair, last_own, last_pair, name="last",
    )[0]

    if blocked:
        gate_far = exchange(add_all(*gate_far, HALF), "fsdp", 2)
        gate_total = add_all(gate_own[0], gate_own[1] + [gate_far], FULL)
        attn_far = exchange(add_all(*attn_far, HALF), "fsdp", 2)
        attn_total = add_all(attn_own[0], attn_own[1] + [attn_far], FULL)
        grad_in = jnp.transpose(gate_total[: 2 * hidden].reshape(2, hidden, LANES), (2, 0, 1))
        grad_down = gate_total[2 * hidden :]
        grad_qkv = attn_total[: 3 * cols].reshape(3, cols // LANES, LANES, LANES)
        grad_qkv = jnp.transpose(grad_qkv, (2, 0, 1, 3)).reshape(LANES, 3, cols)
        grad_out = attn_total[3 * cols :]
    else:

        def summed(far, own, axis):
            far, own = (
                lax.psum_scatter(v, "seq", scatter_dimension=axis, tiled=True) for v in (far, own)
            )
            return own.astype(FULL) + exchange(far, "fsdp", 2).astype(FULL)

        far, own = (
            jnp.transpose(whole_blocks(scalars, *v), (1, 0, 2)).reshape(3 * hidden, width) for v in gate_parts
        )
        gate_total = summed(far, own, 1)
        grad_in = jnp.transpose(gate_total[: 2 * hidden].reshape(2, hidden, -1), (2, 0, 1))
        grad_down = gate_total[2 * hidden :]
        far, own = (whole_blocks(scalars, *v) for v in (attn_far_parts, attn_own_parts))
        grad_out = summed(
            *(jnp.transpose(v[:, 3 * cols :], (1, 0, 2)).reshape(cols, width) for v in (far, own)), 1
        )

        def rows_first(v):
            v = v[:, : 3 * cols].reshape(-1, 3, cols // LANES, LANES, LANES)
            return jnp.transpose(v, (0, 3, 1, 2, 4)).reshape(width, 3, cols)

        grad_qkv = summed(rows_first(far), rows_first(own), 0)

    gains = jnp.concatenate([gsum_one, gsum_two], axis=0)
    for axis, size in (("fsdp", fsdp), ("seq", seq)):
        bit = 1
        while bit < size:
            gains = gains + exchange(gains, axis, bit)
            bit *= 2
    share = width // fsdp
    gains = lax.dynamic_slice_in_dim(gains, column * share, share, 1)
    return (
        result[None],
        grad_input[None],
        grad_qkv,
        grad_out,
        grad_in,
        grad_down,
        gains[0],
        gains[1],
    )


def solution(mesh):
    return jax.shard_map(
        body,
        mesh=mesh,
        in_specs=(
            P("fsdp", "seq", None),
            P(),
            P(),
            P(),
            P(None, None, "fsdp"),
            P("fsdp", None),
            P(None, None, "fsdp"),
            P("fsdp", None),
            P("fsdp", "seq", None),
        ),
        out_specs=(
            P("fsdp", "seq", None),
            P("fsdp", "seq", None),
            P("seq", None, "fsdp"),
            P("fsdp", "seq"),
            P("seq", None, "fsdp"),
            P("fsdp", "seq"),
            P("fsdp"),
            P("fsdp"),
        ),
        check_vma=False,
    )
```
